32 devices in a mesh: blk: 8 (over z, y), tab: 4 (over x, core).
Axes of the slice: x: 2, y: 2, z: 4, core: 2. Of those that a mesh axis runs over, the one named last changes fastest.
Arguments:
- accounts: bfloat16 [65536, 128], P(('blk', 'tab')), may hold values from -0.5 to 0.5
- merchants: bfloat16 [65536, 128], P(('blk', 'tab')), may hold values from -6 to 6
- logit_scale: float32 [1], replicated, may hold values from 1 to 4
- logit_bias: float32 [1], replicated, may hold values from -3 to -1
- positive: int32 [65536], P(('blk', 'tab')), may hold values from 0 to 8191
- account_ids: int32 [65536], P(('blk', 'tab')), may hold values from 0 to 1023
- merchant_ids: int32 [65536], P(('blk', 'tab')), may hold values from 0 to 1023
- account_owner: int32 [512, 1], P(('blk', 'tab')), may hold values from 0 to 3; in each aligned block of 16 rows (0 to 15, 16 to 31, ...) at most 8 rows name the same one
- merchant_owner: int32 [512, 1], P(('blk', 'tab')), may hold values from 0 to 3; in each aligned block of 16 rows (0 to 15, 16 to 31, ...) at most 8 rows name the same one
Outputs:
- account_grad: float32 [32768, 128], P(('blk', 'tab'))
- merchant_grad: float32 [32768, 128], P(('blk', 'tab'))
The draws below stay inside these ranges and needn't reach their ends.
Inputs may be any that keep to these rules, and one draw needn't show every extreme that they name: `account_owner`: among the 16 row blocks of one batch block at most 8 have the same owner, and some batch block gives exactly 8 to one owner. `merchant_owner`: among the 16 row blocks of one batch block at most 8 have the same owner, and some batch block gives exactly 8 to one owner.
All inputs are finite; a program needn't handle non-finite values.
Results may differ from the reference program's by a relative error of at most 0.00048.
Values may be sent and summed in bfloat16 or wider, within the bound.
A program may use at most 64 MiB of HBM per device.

```python
import math
import jax
import jax.numpy as jnp
import numpy as np
from jax import lax

D = 128
A_DEV = 2048
STEPS = 4
BLOCK_ROWS = 128
TROWS = 1024
BLOCKS_DEV = 16
CAP = 8
ROWS = 65536
N_BLK = 8
N_TAB = 4


def plant(entries, rng, low, largest):
    shape = entries.shape
    place = [jax.random.randint(jax.random.fold_in(rng, axis), (), 0, shape[axis]) for axis in range(len(shape))]
    entries = entries.at[tuple(place)].set(low)
    longest = shape.index(max(shape))
    place[longest] = (place[longest] + 1) % shape[longest]
    return entries.at[tuple(place)].set(largest)


def level_of(key, dims, cuts, low, high):
    loudness = 1.0
    for axis_at, shards_of in cuts:
        draws = jax.random.uniform(jax.random.fold_in(jax.random.fold_in(key, 6), axis_at), (shards_of,), jnp.float32, low / len(cuts), high / len(cuts))
        loudness = loudness * jnp.repeat(jnp.exp(draws), dims[axis_at] // shards_of).reshape((-1,) + (1,) * (len(dims) - 1 - axis_at))
    return loudness


def cumulative_ranks(amount, slope):
    weights = [(1 << 20) // math.isqrt(standing ** slope) + 1 for standing in range(1, amount + 1)]
    spread = 1 + sum(weights) // (1 << 30)
    return np.cumsum(np.array([max(1, weight // spread) for weight in weights]))


def ranked(rng, extent, count, lean):
    listing = cumulative_ranks(count, lean)
    pick = jax.random.randint(jax.random.fold_in(rng, 1), extent, 0, int(listing[count - 1]))
    standing = jnp.searchsorted(jnp.asarray(listing, jnp.int32), pick, side="right")
    return jax.random.permutation(jax.random.fold_in(rng, 2), count)[standing].astype(jnp.int32)


def deal_out(rng, own, number, rows, count, top, bound, skew):
    sequence = jax.random.permutation(rng, count)
    crowded, common = load_shares(count, rows * top, bound, skew, True), load_shares(count, rows * top, bound, skew, False)
    places = jnp.arange(count)

    def named(tallies, offset_by):
        used = int((tallies > 0).sum())
        fixed = max(1, used // 4)
        moved = fixed + (places - fixed + offset_by * (used - fixed)) % max(1, count - fixed)
        return jnp.zeros((count,), jnp.int32).at[sequence[jnp.where(places < fixed, places, moved)]].set(jnp.asarray(tallies, jnp.int32))

    tallies = jnp.where(number % 4 == 0, named(crowded, number // 4), named(common, number - number // 4 - 1))
    mixed = jax.random.permutation(jax.random.fold_in(own, 3), count)
    source_of, sink = mixed[0:count // 2 * 2:2], mixed[1:count // 2 * 2:2]
    room = jnp.minimum(tallies[source_of] - 1, bound - tallies[sink]) // 2
    room = jnp.where((source_of == sequence[0]) | (sink == sequence[0]) | (tallies[sink] == 0), 0, jnp.maximum(room, 0))
    moved = jax.random.randint(jax.random.fold_in(own, 4), (count // 2,), 0, 1 << 20) % (room + 1)
    tallies = tallies.at[source_of].add(-moved).at[sink].add(moved)
    items = jnp.searchsorted(jnp.cumsum(tallies), jnp.arange(rows * top), side="right").astype(jnp.int32)
    table = items.reshape(top, rows).T
    table = table[jax.random.permutation(jax.random.fold_in(own, 1), rows)]
    offset_by = jax.random.randint(jax.random.fold_in(own, 2), (rows, 1), 0, top)
    return jnp.take_along_axis(table, (jnp.arange(top)[None, :] + offset_by) % top, axis=1)


def load_shares(amount, total, bound, slope, full):
    portions = [(1 << 20) // math.isqrt(grade ** slope) + 1 for grade in range(1, amount + 1)]
    largest = bound if full else min(bound, max(-(-total // amount), total * portions[0] // sum(portions)))
    least = 1 if total - largest >= amount - 1 else 0
    holding, spare = [largest] + [least] * (amount - 1), total - largest - least * (amount - 1)
    while spare > 0:
        free = [i for i in range(1, amount) if holding[i] < largest] or [i for i in range(1, amount) if holding[i] < bound]
        pool, left = sum([portions[i] for i in free]), spare
        for i in free:
            extra = min(bound - holding[i], max(1, left * portions[i] // pool), spare)
            holding[i] = holding[i] + extra
            spare = spare - extra
    return np.array(holding)


def noise(rng, dims, deviation, most, cuts=(), held_as=jnp.bfloat16):
    drawn = deviation * jax.random.normal(rng, dims, jnp.float32)
    if cuts:
        drawn = drawn * level_of(rng, dims, cuts, -0.22, 0.18)
    return jnp.clip(drawn, -most, most).astype(held_as)


def setup_inputs(seed: int = 0) -> dict:
    streams_of = jax.random.split(jax.random.key(seed), 10)
    accounts = noise(streams_of[0], (ROWS, D), D ** -0.5, 0.5, ((0, 32),))
    merchants = noise(streams_of[1], (ROWS, D), 1.0, 6.0, ((0, 32),))
    logit_scale = jnp.clip(jnp.exp(jax.random.uniform(streams_of[2], (1,), jnp.float32, math.log(1.0), math.log(4.0))), 1.0, 4.0)
    logit_bias = jnp.clip(jax.random.uniform(streams_of[3], (1,), jnp.float32, -3.0, -1.0), -3.0, -1.0)
    positive = plant(jax.random.randint(streams_of[4], (ROWS,), 0, STEPS * A_DEV), jax.random.fold_in(streams_of[4], 1), 0, (STEPS * A_DEV) - 1).astype(jnp.int32)
    account_ids = plant(ranked(streams_of[5], (ROWS,), TROWS, 2), jax.random.fold_in(streams_of[5], 3), 0, TROWS - 1).astype(jnp.int32)
    merchant_ids = plant(ranked(streams_of[6], (ROWS,), TROWS, 2), jax.random.fold_in(streams_of[6], 3), 0, TROWS - 1).astype(jnp.int32)
    account_owner_keys = jax.random.split(jax.random.fold_in(streams_of[7], 1), (N_BLK * N_TAB * BLOCKS_DEV) // BLOCKS_DEV)
    account_owner_turns = jax.random.permutation(jax.random.fold_in(streams_of[7], 3), (N_BLK * N_TAB * BLOCKS_DEV) // BLOCKS_DEV)
    account_owner = jax.vmap(lambda own, number: deal_out(jax.random.fold_in(streams_of[7], 2), own, number, BLOCKS_DEV, N_TAB, 1, CAP, 2))(account_owner_keys, account_owner_turns).reshape((N_BLK * N_TAB * BLOCKS_DEV, 1))
    merchant_owner_keys = jax.random.split(jax.random.fold_in(streams_of[8], 1), (N_BLK * N_TAB * BLOCKS_DEV) // BLOCKS_DEV)
    merchant_owner_turns = jax.random.permutation(jax.random.fold_in(streams_of[8], 3), (N_BLK * N_TAB * BLOCKS_DEV) // BLOCKS_DEV)
    merchant_owner = jax.vmap(lambda own, number: deal_out(jax.random.fold_in(streams_of[8], 2), own, number, BLOCKS_DEV, N_TAB, 1, CAP, 2))(merchant_owner_keys, merchant_owner_turns).reshape((N_BLK * N_TAB * BLOCKS_DEV, 1))
    return {"accounts": accounts, "merchants": merchants, "logit_scale": logit_scale, "logit_bias": logit_bias, "positive": positive, "account_ids": account_ids, "merchant_ids": merchant_ids, "account_owner": account_owner, "merchant_owner": merchant_owner}


def tile_grads(acc_block, merch_block, relative, offset, scale, bias):
    row_step = min(512, A_DEV)
    count = acc_block.shape[0] // row_step
    pieces = acc_block.reshape(count, row_step, D)
    labels = relative.reshape(count, row_step)
    columns = offset + jnp.arange(merch_block.shape[0], dtype=jnp.int32)

    def one_block(carry, item):
        piece, label = item
        logits = scale * lax.dot_general(piece, merch_block, (((1,), (1,)), ((), ())), preferred_element_type=jnp.float32) + bias
        signs = jnp.where(label[:, None] == columns[None, :], jnp.float32(1.0), jnp.float32(-1.0))
        delta = (-signs * jax.nn.sigmoid(-signs * logits)).astype(jnp.bfloat16)
        grad_rows = scale * jnp.dot(delta, merch_block, preferred_element_type=jnp.float32)
        merch_part = carry + scale * lax.dot_general(delta, piece, (((0,), (0,)), ((), ())), preferred_element_type=jnp.float32)
        return merch_part, grad_rows

    start = jnp.zeros((merch_block.shape[0], D), jnp.float32)
    merch_grad, acc_grad = lax.scan(one_block, start, (pieces, labels))
    return acc_grad.reshape(-1, D), merch_grad


def table_sum(grads, ids, owner):
    devices = N_BLK * N_TAB
    owner_rows = jnp.repeat(owner.reshape(devices, A_DEV // BLOCK_ROWS), BLOCK_ROWS, axis=1).reshape(-1)
    group = jnp.repeat(jnp.arange(devices, dtype=jnp.int32) // N_TAB, A_DEV)
    target = ((group * N_TAB + owner_rows) * TROWS + ids).astype(jnp.int32)
    return jax.ops.segment_sum(grads, target, num_segments=devices * TROWS)


def reference(accounts, merchants, logit_scale, logit_bias, positive, account_ids, merchant_ids, account_owner, merchant_owner):
    devices = N_BLK * N_TAB
    scale = logit_scale[0]
    bias = logit_bias[0]
    acc_four = accounts.reshape(N_BLK, N_TAB, A_DEV, D)
    merch_four = merchants.reshape(N_BLK, N_TAB, A_DEV, D)
    labels = positive.reshape(devices, A_DEV)
    acc_total = jnp.zeros((N_BLK, N_TAB, A_DEV, D), jnp.float32)
    merch_total = jnp.zeros((N_BLK, N_TAB, A_DEV, D), jnp.float32)
    for cycle_step in range(STEPS):
        partner = jnp.roll(merch_four, cycle_step, axis=0).reshape(devices, A_DEV, D)

        def per_block(item, cycle_step=cycle_step):
            return tile_grads(item[0], item[1], item[2], cycle_step * A_DEV, scale, bias)

        acc_part, merch_part = lax.map(per_block, (acc_four.reshape(devices, A_DEV, D), partner, labels))
        acc_total = acc_total + acc_part.reshape(N_BLK, N_TAB, A_DEV, D)
        merch_total = merch_total + jnp.roll(merch_part.reshape(N_BLK, N_TAB, A_DEV, D), -cycle_step, axis=0)
    account_grad = table_sum(acc_total.reshape(-1, D), account_ids, account_owner)
    merchant_grad = table_sum(merch_total.reshape(-1, D), merchant_ids, merchant_owner)
    return account_grad, merchant_grad
```

```python
import functools

import jax
import jax.numpy as jnp
from jax import lax
from jax.experimental import pallas as pl
from jax.experimental.pallas import tpu as pltpu
from jax.sharding import PartitionSpec as P

STEPS = 4
BLOCK_ROWS = 128
TROWS = 1024
ROW_STEP = 512
COL_STEP = 512
MESH = pl.DeviceIdType.MESH


def kernel(
    n_blk,
    acc_in, merch_in, pos_in, acc_ids, merch_ids, acc_own, merch_own, scale_in, bias_in,
    acc_out, merch_out,
    guests_m, guests_a, guests_l, label_cols, grad_a, grad_m, split_a, split_m, keys_a, keys_m,
    pair_send, pair_recv, far_send, far_recv,
    send_m, recv_m, send_a, recv_a, send_l, recv_l,
    pair_ssem, pair_rsem, far_ssem, far_rsem,
):
    rows, width = acc_in.shape
    blocks = rows // BLOCK_ROWS
    row_step, col_step = min(ROW_STEP, rows), min(COL_STEP, rows)
    i, k = lax.axis_index("blk"), lax.axis_index("tab")
    odd = lax.rem(i, 2)
    even = 1 - odd
    up, down = lax.rem(i + 2, n_blk), lax.rem(i + n_blk - 2, n_blk)
    beside = i + 1 - 2 * odd
    core_bit, far_bit = lax.rem(k, 2), k // 2
    pair = far_bit * 2 + 1 - core_bit
    far = (1 - far_bit) * 2 + core_bit
    cross = (1 - far_bit) * 2 + 1 - core_bit
    half_scale = scale_in[0] * 0.5
    half_bias = bias_in[0] * 0.5

    barrier = pltpu.get_barrier_semaphore()
    for there in ((up, k), (down, k), (beside, k), (i, pair), (i, far)):
        pl.semaphore_signal(barrier, inc=1, device_id=there, device_id_type=MESH)
    pl.semaphore_wait(barrier, 5)

    def send(src, dst, ssem, rsem, there):
        return pltpu.make_async_remote_copy(
            src_ref=src, dst_ref=dst, send_sem=ssem, recv_sem=rsem, device_id=there, device_id_type=MESH
        )

    def merch_copy(src, hop, slot, there):
        return (send(src, guests_m.at[slot], send_m.at[hop], recv_m.at[slot], there),)

    def acc_copy(src, labels, hop, slot, there):
        return (
            send(src, guests_a.at[slot], send_a.at[hop], recv_a.at[slot], there),
            send(labels, guests_l.at[slot], send_l.at[hop], recv_l.at[slot], there),
        )

    def start(copies):
        for copy in copies:
            copy.start()

    m_hops = (
        merch_copy(merch_in, 0, 1, (up, k)),
        merch_copy(merch_in, 1, 0, (beside, k)),
        merch_copy(guests_m.at[1], 2, 2 * even, (beside, k)),
        merch_copy(guests_m.at[0], 3, 2, (up, k)),
    )
    a_hops = (
        acc_copy(acc_in, pos_in, 0, 1, (down, k)),
        acc_copy(acc_in, pos_in, 1, 0, (beside, k)),
        acc_copy(guests_a.at[1], guests_l.at[1], 2, 2 * odd, (beside, k)),
        acc_copy(guests_a.at[0], guests_l.at[0], 3, 2, (down, k)),
    )

    def arrived_m(slot):
        send(guests_m.at[slot], guests_m.at[slot], send_m.at[0], recv_m.at[slot], (up, k)).wait_recv()

    def arrived_a(slot):
        send(guests_a.at[slot], guests_a.at[slot], send_a.at[0], recv_a.at[slot], (up, k)).wait_recv()
        send(guests_l.at[slot], guests_l.at[slot], send_l.at[0], recv_l.at[slot], (up, k)).wait_recv()

    start(m_hops[0])
    start(a_hops[0])

    @pl.when(odd == 0)
    def _():
        start(m_hops[1])

    @pl.when(odd == 1)
    def _():
        start(a_hops[1])

    for block in range(blocks):
        column = jnp.broadcast_to(pos_in[block : block + 1, :], (BLOCK_ROWS, BLOCK_ROWS)).T
        label_cols[block * BLOCK_ROWS : (block + 1) * BLOCK_ROWS, :] = column
    keys_a[...] = acc_own[...] * TROWS + acc_ids[...]
    keys_m[...] = merch_own[...] * TROWS + merch_ids[...]

    def flat(ref, first, count):
        return jnp.concatenate([ref[first + j : first + j + 1, :] for j in range(count)], axis=1)

    def delta_of(mine, theirs, hit):
        logits = lax.dot_general(mine, theirs, (((1,), (1,)), ((), ())), preferred_element_type=jnp.float32)
        raised = jnp.tanh(logits * half_scale + half_bias)
        return (raised + jnp.where(hit, jnp.float32(-1.0), jnp.float32(1.0))).astype(jnp.bfloat16)

    def tile(mine, theirs, grad, first, hits):
        def piece(p, carry):
            at = pl.multiple_of(p * row_step, row_step)
            own = mine[pl.ds(at, row_step), :]
            total = jnp.zeros((row_step, width), jnp.float32)
            for c in range(0, rows, col_step):
                other = theirs[pl.ds(c, col_step), :]
                total = total + jnp.dot(
                    delta_of(own, other, hits(at, c)), other, preferred_element_type=jnp.float32
                )
            if first:
                grad[pl.ds(at, row_step), :] = total
            else:
                grad[pl.ds(at, row_step), :] += total
            return carry

        lax.fori_loop(0, rows // row_step, piece, 0)

    def acc_tile(s):
        lane = lax.broadcasted_iota(jnp.int32, (row_step, col_step), 1)

        def hits(at, c):
            labels = label_cols[pl.ds(at, row_step), :] - (s * rows + c)
            return jnp.concatenate([labels] * (col_step // BLOCK_ROWS), axis=1) == lane

        tile(acc_in, merch_in if s == 0 else guests_m.at[s - 1], grad_a, s == 0, hits)

    def merch_tile(s):
        row = lax.broadcasted_iota(jnp.int32, (row_step, col_step), 0)
        labels = pos_in if s == 0 else guests_l.at[s - 1]

        def hits(at, c):
            line = flat(labels, c // BLOCK_ROWS, col_step // BLOCK_ROWS) - (s * rows + at)
            return line == row

        tile(merch_in, acc_in if s == 0 else guests_a.at[s - 1], grad_m, s == 0, hits)

    def split(grad, pieces):
        def one(p, carry):
            at = pl.multiple_of(p * 256, 256)
            value = grad[pl.ds(at, 256), :] * half_scale
            high = value.astype(jnp.bfloat16)
            pieces[pl.ds(at, 256), 0:width] = high
            pieces[pl.ds(at, 256), width : 2 * width] = (value - high.astype(jnp.float32)).astype(jnp.bfloat16)
            return carry

        lax.fori_loop(0, rows // 256, one, 0)

    def table(pieces, keys, owner, put):
        step = 512

        def one(p, carry):
            at = pl.multiple_of(p * step, step)
            total = jnp.zeros((step, 2 * width), jnp.float32)
            row = lax.broadcasted_iota(jnp.int32, (step, col_step), 0)
            for c in range(0, rows, col_step):
                line = flat(keys, c // BLOCK_ROWS, col_step // BLOCK_ROWS) - (owner * TROWS + at)
                named = jnp.where(line == row, jnp.float32(1.0), jnp.float32(0.0)).astype(jnp.bfloat16)
                total = total + jnp.dot(
                    named, pieces[pl.ds(c, col_step), :], preferred_element_type=jnp.float32
                )
            put(pl.ds(at, step), total[:, 0:width] + total[:, width : 2 * width])
            return carry

        lax.fori_loop(0, TROWS // step, one, 0)

    def storing(ref):
        def put(at, value):
            ref[at, :] = value

        return put

    def pair_copy(side, turn):
        return send(
            pair_send.at[side, turn], pair_recv.at[side, turn], pair_ssem.at[side, turn],
            pair_rsem.at[side, turn], (i, pair),
        )

    def far_copy(side):
        return send(far_send.at[side], far_recv.at[side], far_ssem.at[side], far_rsem.at[side], (i, far))

    def give(side, pieces, keys):
        table(pieces, keys, cross, storing(pair_send.at[side, 0]))
        pair_copy(side, 0).start()
        table(pieces, keys, far, storing(far_send.at[side]))
        pair_copy(side, 0).wait_recv()
        far_send[side] = far_send[side] + pair_recv[side, 0]
        far_copy(side).start()

    acc_tile(0)
    merch_tile(0)
    arrived_m(1)
    start(m_hops[2])
    arrived_a(1)
    start(a_hops[2])
    acc_tile(2)
    merch_tile(2)
    arrived_m(0)

    @pl.when(odd == 0)
    def _():
        start(m_hops[3])

    arrived_a(0)

    @pl.when(odd == 1)
    def _():
        start(a_hops[3])

    acc_tile(1)
    merch_tile(1)
    arrived_m(2)
    acc_tile(3)
    split(grad_a, split_a)
    give(0, split_a, keys_a)
    arrived_a(2)
    merch_tile(3)
    split(grad_m, split_m)
    give(1, split_m, keys_m)
    sides = ((0, split_a, keys_a, acc_out), (1, split_m, keys_m, merch_out))
    for side, pieces, keys, out in sides:
        table(pieces, keys, pair, storing(pair_send.at[side, 1]))
        pair_copy(side, 1).start()
    for side, pieces, keys, out in sides:
        table(pieces, keys, k, storing(out))
    for side, pieces, keys, out in sides:
        pair_copy(side, 1).wait_recv()
        far_copy(side).wait_recv()
        out[...] = out[...] + pair_recv[side, 1] + far_recv[side]
        pair_copy(side, 0).wait_send()
        pair_copy(side, 1).wait_send()
        far_copy(side).wait_send()

    def drain(copies):
        for copy in copies:
            copy.wait_send()

    drain(m_hops[0] + m_hops[2] + a_hops[0] + a_hops[2])

    @pl.when(odd == 0)
    def _():
        drain(m_hops[1] + m_hops[3])

    @pl.when(odd == 1)
    def _():
        drain(a_hops[1] + a_hops[3])


def per_device(
    n_blk, accounts, merchants, logit_scale, logit_bias, positive,
    account_ids, merchant_ids, account_owner, merchant_owner,
):
    rows, width = accounts.shape
    blocks = rows // BLOCK_ROWS
    vmem = pl.BlockSpec(memory_space=pltpu.VMEM)
    smem = pl.BlockSpec(memory_space=pltpu.SMEM)
    guests = STEPS - 1
    table = jax.ShapeDtypeStruct((TROWS, width), jnp.float32)
    grid_of = lambda x: x.reshape(blocks, BLOCK_ROWS)
    return pl.pallas_call(
        functools.partial(kernel, n_blk),
        out_shape=(table, table),
        in_specs=[vmem] * 7 + [smem] * 2,
        out_specs=(vmem, vmem),
        scratch_shapes=[
            pltpu.VMEM((guests, rows, width), jnp.bfloat16),
            pltpu.VMEM((guests, rows, width), jnp.bfloat16),
            pltpu.VMEM((guests, blocks, BLOCK_ROWS), jnp.int32),
            pltpu.VMEM((rows, BLOCK_ROWS), jnp.int32),
            pltpu.VMEM((rows, width), jnp.float32),
            pltpu.VMEM((rows, width), jnp.float32),
            pltpu.VMEM((rows, 2 * width), jnp.bfloat16),
            pltpu.VMEM((rows, 2 * width), jnp.bfloat16),
            pltpu.VMEM((blocks, BLOCK_ROWS), jnp.int32),
            pltpu.VMEM((blocks, BLOCK_ROWS), jnp.int32),
            pltpu.VMEM((2, 2, TROWS, width), jnp.float32),
            pltpu.VMEM((2, 2, TROWS, width), jnp.float32),
            pltpu.VMEM((2, TROWS, width), jnp.float32),
            pltpu.VMEM((2, TROWS, width), jnp.float32),
            pltpu.SemaphoreType.DMA((4,)),
            pltpu.SemaphoreType.DMA((guests,)),
            pltpu.SemaphoreType.DMA((4,)),
            pltpu.SemaphoreType.DMA((guests,)),
            pltpu.SemaphoreType.DMA((4,)),
            pltpu.SemaphoreType.DMA((guests,)),
            pltpu.SemaphoreType.DMA((2, 2)),
            pltpu.SemaphoreType.DMA((2, 2)),
            pltpu.SemaphoreType.DMA((2,)),
            pltpu.SemaphoreType.DMA((2,)),
        ],
        compiler_params=pltpu.CompilerParams(
            collective_id=0, has_side_effects=True, vmem_limit_bytes=60 * 1024 * 1024
        ),
        name="two_tower",
    )(
        accounts, merchants, grid_of(positive), grid_of(account_ids), grid_of(merchant_ids),
        account_owner, merchant_owner, logit_scale, logit_bias,
    )


def solution(mesh):
    return jax.shard_map(
        functools.partial(per_device, mesh.shape["blk"]),
        mesh=mesh,
        in_specs=(
            P(("blk", "tab"), None),
            P(("blk", "tab"), None),
            P(),
            P(),
            P(("blk", "tab")),
            P(("blk", "tab")),
            P(("blk", "tab")),
            P(("blk", "tab"), None),
            P(("blk", "tab"), None),
        ),
        out_specs=(P(("blk", "tab"), None), P(("blk", "tab"), None)),
        check_vma=False,
    )
```

```python
import functools

import jax
import jax.numpy as jnp
from jax import lax
from jax.experimental import pallas as pl
from jax.experimental.pallas import tpu as pltpu
from jax.sharding import PartitionSpec as P

STEPS = 4
BLOCK_ROWS = 128
TROWS = 1024
ROW_STEP = 1024
COL_STEP = 256
MESH = pl.DeviceIdType.MESH


def kernel(
    n_blk,
    acc_in, merch_in, pos_in, acc_ids, merch_ids, acc_own, merch_own, scale_in, bias_in,
    acc_out, merch_out,
    guests_m, guests_a, guests_l, label_cols, grad_a, grad_m, split_a, split_m, keys_a, keys_m,
    pair_send, pair_recv, far_send, far_recv,
    send_m, recv_m, send_a, recv_a, send_l, recv_l,
    pair_ssem, pair_rsem, far_ssem, far_rsem,
):
    rows, width = acc_in.shape
    blocks = rows // BLOCK_ROWS
    row_step, col_step = min(ROW_STEP, rows), min(COL_STEP, rows)
    i, k = lax.axis_index("blk"), lax.axis_index("tab")
    odd = lax.rem(i, 2)
    even = 1 - odd
    up, down = lax.rem(i + 2, n_blk), lax.rem(i + n_blk - 2, n_blk)
    beside = i + 1 - 2 * odd
    core_bit, far_bit = lax.rem(k, 2), k // 2
    pair = far_bit * 2 + 1 - core_bit
    far = (1 - far_bit) * 2 + core_bit
    cross = (1 - far_bit) * 2 + 1 - core_bit
    half_scale = scale_in[0] * 0.5
    half_bias = bias_in[0] * 0.5

    barrier = pltpu.get_barrier_semaphore()
    for there in ((up, k), (down, k), (beside, k), (i, pair), (i, far)):
        pl.semaphore_signal(barrier, inc=1, device_id=there, device_id_type=MESH)
    pl.semaphore_wait(barrier, 5)

    def send(src, dst, ssem, rsem, there):
        return pltpu.make_async_remote_copy(
            src_ref=src, dst_ref=dst, send_sem=ssem, recv_sem=rsem, device_id=there, device_id_type=MESH
        )

    half = rows // 2

    def merch_copy(src, hop, slot, there):
        return [
            (send(src.at[part], guests_m.at[slot, part], send_m.at[hop, h], recv_m.at[slot, h], there),)
            for h, part in enumerate((pl.ds(0, half), pl.ds(half, half)))
        ]

    def acc_copy(src, labels, hop, slot, there):
        whole = (send(labels, guests_l.at[slot], send_l.at[hop], recv_l.at[slot], there),)
        return [
            (send(src.at[part], guests_a.at[slot, part], send_a.at[hop, h], recv_a.at[slot, h], there),)
            + (whole if h == 0 else ())
            for h, part in enumerate((pl.ds(0, half), pl.ds(half, half)))
        ]

    def start(copies):
        for copy in copies:
            copy.start()

    m_hops = (
        merch_copy(merch_in, 0, 1, (up, k)),
        merch_copy(merch_in, 1, 0, (beside, k)),
        merch_copy(guests_m.at[1], 2, 2 * even, (beside, k)),
        merch_copy(guests_m.at[0], 3, 2, (up, k)),
    )
    a_hops = (
        acc_copy(acc_in, pos_in, 0, 1, (down, k)),
        acc_copy(acc_in, pos_in, 1, 0, (beside, k)),
        acc_copy(guests_a.at[1], guests_l.at[1], 2, 2 * odd, (beside, k)),
        acc_copy(guests_a.at[0], guests_l.at[0], 3, 2, (down, k)),
    )

    def arrived_m(slot, h):
        part = guests_m.at[slot, pl.ds(h * half, half)]
        send(part, part, send_m.at[0, h], recv_m.at[slot, h], (up, k)).wait_recv()

    def arrived_a(slot, h):
        part = guests_a.at[slot, pl.ds(h * half, half)]
        send(part, part, send_a.at[0, h], recv_a.at[slot, h], (up, k)).wait_recv()
        if h == 0:
            send(guests_l.at[slot], guests_l.at[slot], send_l.at[0], recv_l.at[slot], (up, k)).wait_recv()

    def pass_m(h):
        arrived_m(0, h)

        @pl.when(odd == 0)
        def _():
            start(m_hops[3][h])

    def pass_a(h):
        arrived_a(0, h)

        @pl.when(odd == 1)
        def _():
            start(a_hops[3][h])

    for h in range(2):
        start(m_hops[0][h])
        start(a_hops[0][h])

        @pl.when(odd == 0)
        def _():
            start(m_hops[1][h])

        @pl.when(odd == 1)
        def _():
            start(a_hops[1][h])

    grad_a[...] = jnp.zeros_like(grad_a)
    grad_m[...] = jnp.zeros_like(grad_m)
    for block in range(blocks):
        column = jnp.broadcast_to(pos_in[block : block + 1, :], (BLOCK_ROWS, BLOCK_ROWS)).T
        label_cols[block * BLOCK_ROWS : (block + 1) * BLOCK_ROWS, :] = column
    for block in range(blocks):
        here = slice(block, block + 1)
        keys_a[here, :] = acc_own[:, here] * TROWS + acc_ids[here, :]
        keys_m[here, :] = merch_own[:, here] * TROWS + merch_ids[here, :]

    def flat(ref, first, count):
        return jnp.concatenate([ref[first + j : first + j + 1, :] for j in range(count)], axis=1)

    def logits_of(mine, theirs):
        return lax.dot_general(mine, theirs, (((1,), (1,)), ((), ())), preferred_element_type=jnp.float32)

    def delta_of(logits, hit):
        raised = jnp.tanh(logits * half_scale + half_bias)
        return (raised + jnp.where(hit, jnp.float32(-1.0), jnp.float32(1.0))).astype(jnp.bfloat16)

    def tile(mine, theirs, grad, hits):
        chunks = theirs.shape[0] // col_step
        together = 2 if rows % (2 * row_step) == 0 else 1

        def pieces(p, carry):
            for q in range(together):
                at = pl.multiple_of((p * together + q) * row_step, row_step)
                own = mine[pl.ds(at, row_step), :]
                total = jnp.zeros((row_step, width), jnp.float32)
                for c in range(0, chunks * col_step, col_step):
                    other = theirs[pl.ds(c, col_step), :]
                    delta = delta_of(logits_of(own, other), hits(at, c))
                    total = total + jnp.dot(delta, other, preferred_element_type=jnp.float32)
                grad[pl.ds(at, row_step), :] += total
            return carry

        lax.fori_loop(0, rows // (together * row_step), pieces, 0)

    def acc_tile(s, first=0, span=rows):
        lane = lax.broadcasted_iota(jnp.int32, (row_step, col_step), 1)

        def hits(at, c):
            labels = label_cols[pl.ds(at, row_step), :] - (s * rows + first + c)
            return jnp.concatenate([labels] * (col_step // BLOCK_ROWS), axis=1) == lane

        theirs = merch_in if s == 0 else guests_m.at[s - 1]
        tile(acc_in, theirs.at[pl.ds(first, span)], grad_a, hits)

    def merch_tile(s, first=0, span=rows):
        row = lax.broadcasted_iota(jnp.int32, (row_step, col_step), 0)
        labels = pos_in if s == 0 else guests_l.at[s - 1]

        def hits(at, c):
            line = flat(labels, (first + c) // BLOCK_ROWS, col_step // BLOCK_ROWS) - (s * rows + at)
            return line == row

        theirs = acc_in if s == 0 else guests_a.at[s - 1]
        tile(merch_in, theirs.at[pl.ds(first, span)], grad_m, hits)

    def split(grad, pieces):
        def one(p, carry):
            at = pl.multiple_of(p * 256, 256)
            value = grad[pl.ds(at, 256), :] * half_scale
            high = value.astype(jnp.bfloat16)
            pieces[pl.ds(at, 256), 0:width] = high
            pieces[pl.ds(at, 256), width : 2 * width] = (value - high.astype(jnp.float32)).astype(jnp.bfloat16)
            return carry

        lax.fori_loop(0, rows // 256, one, 0)

    def table(pieces, keys, owner, put):
        step = 512

        def one(p, carry):
            at = pl.multiple_of(p * step, step)
            total = jnp.zeros((step, 2 * width), jnp.float32)
            row = lax.broadcasted_iota(jnp.int32, (step, col_step), 0)
            for c in range(0, rows, col_step):
                line = flat(keys, c // BLOCK_ROWS, col_step // BLOCK_ROWS) - (owner * TROWS + at)
                named = jnp.where(line == row, jnp.float32(1.0), jnp.float32(0.0)).astype(jnp.bfloat16)
                total = total + jnp.dot(
                    named, pieces[pl.ds(c, col_step), :], preferred_element_type=jnp.float32
                )
            put(pl.ds(at, step), total[:, 0:width] + total[:, width : 2 * width])
            return carry

        lax.fori_loop(0, TROWS // step, one, 0)

    def storing(ref):
        def put(at, value):
            ref[at, :] = value

        return put

    def pair_copy(side, turn):
        return send(
            pair_send.at[side, turn], pair_recv.at[side, turn], pair_ssem.at[side, turn],
            pair_rsem.at[side, turn], (i, pair),
        )

    def far_copy(side):
        return send(far_send.at[side], far_recv.at[side], far_ssem.at[side], far_rsem.at[side], (i, far))

    def give(side, pieces, keys):
        table(pieces, keys, cross, storing(pair_send.at[side, 0]))
        pair_copy(side, 0).start()
        table(pieces, keys, far, storing(far_send.at[side]))
        pair_copy(side, 0).wait_recv()
        far_send[side] = far_send[side] + pair_recv[side, 0]
        far_copy(side).start()

    acc_tile(0)
    merch_tile(0)
    for h in range(2):
        arrived_m(1, h)
        start(m_hops[2][h])
        arrived_a(1, h)
        start(a_hops[2][h])
        acc_tile(2, h * half, half)
        if h == 1:
            pass_m(0)
            pass_a(0)
        merch_tile(2, h * half, half)
    pass_m(1)
    acc_tile(1)
    pass_a(1)
    merch_tile(1)
    arrived_m(2, 0)
    arrived_m(2, 1)
    acc_tile(3)
    split(grad_a, split_a)
    give(0, split_a, keys_a)
    arrived_a(2, 0)
    arrived_a(2, 1)
    merch_tile(3)
    split(grad_m, split_m)
    give(1, split_m, keys_m)
    sides = ((0, split_a, keys_a, acc_out), (1, split_m, keys_m, merch_out))
    for side, pieces, keys, out in sides:
        table(pieces, keys, pair, storing(pair_send.at[side, 1]))
        pair_copy(side, 1).start()
    for side, pieces, keys, out in sides:
        table(pieces, keys, k, storing(out))
    for side, pieces, keys, out in sides:
        pair_copy(side, 1).wait_recv()
        far_copy(side).wait_recv()
        out[...] = out[...] + pair_recv[side, 1] + far_recv[side]
        pair_copy(side, 0).wait_send()
        pair_copy(side, 1).wait_send()
        far_copy(side).wait_send()

    def drain(hop):
        for copy in hop[0] + hop[1]:
            copy.wait_send()

    for hop in (m_hops[0], m_hops[2], a_hops[0], a_hops[2]):
        drain(hop)

    @pl.when(odd == 0)
    def _():
        drain(m_hops[1])
        drain(m_hops[3])

    @pl.when(odd == 1)
    def _():
        drain(a_hops[1])
        drain(a_hops[3])


def per_device(
    n_blk, accounts, merchants, logit_scale, logit_bias, positive,
    account_ids, merchant_ids, account_owner, merchant_owner,
):
    rows, width = accounts.shape
    blocks = rows // BLOCK_ROWS
    vmem = pl.BlockSpec(memory_space=pltpu.VMEM)
    smem = pl.BlockSpec(memory_space=pltpu.SMEM)
    guests = STEPS - 1
    table = jax.ShapeDtypeStruct((TROWS, width), jnp.float32)
    grid_of = lambda x: x.reshape(blocks, BLOCK_ROWS)
    return pl.pallas_call(
        functools.partial(kernel, n_blk),
        out_shape=(table, table),
        in_specs=[vmem] * 7 + [smem] * 2,
        out_specs=(vmem, vmem),
        scratch_shapes=[
            pltpu.VMEM((guests, rows, width), jnp.bfloat16),
            pltpu.VMEM((guests, rows, width), jnp.bfloat16),
            pltpu.VMEM((guests, blocks, BLOCK_ROWS), jnp.int32),
            pltpu.VMEM((rows, BLOCK_ROWS), jnp.int32),
            pltpu.VMEM((rows, width), jnp.float32),
            pltpu.VMEM((rows, width), jnp.float32),
            pltpu.VMEM((rows, 2 * width), jnp.bfloat16),
            pltpu.VMEM((rows, 2 * width), jnp.bfloat16),
            pltpu.VMEM((blocks, BLOCK_ROWS), jnp.int32),
            pltpu.VMEM((blocks, BLOCK_ROWS), jnp.int32),
            pltpu.VMEM((2, 2, TROWS, width), jnp.float32),
            pltpu.VMEM((2, 2, TROWS, width), jnp.float32),
            pltpu.VMEM((2, TROWS, width), jnp.float32),
            pltpu.VMEM((2, TROWS, width), jnp.float32),
            pltpu.SemaphoreType.DMA((4, 2)),
            pltpu.SemaphoreType.DMA((guests, 2)),
            pltpu.SemaphoreType.DMA((4, 2)),
            pltpu.SemaphoreType.DMA((guests, 2)),
            pltpu.SemaphoreType.DMA((4,)),
            pltpu.SemaphoreType.DMA((guests,)),
            pltpu.SemaphoreType.DMA((2, 2)),
            pltpu.SemaphoreType.DMA((2, 2)),
            pltpu.SemaphoreType.DMA((2,)),
            pltpu.SemaphoreType.DMA((2,)),
        ],
        compiler_params=pltpu.CompilerParams(
            collective_id=0, has_side_effects=True, vmem_limit_bytes=60 * 1024 * 1024
        ),
        name="two_tower",
    )(
        accounts, merchants, grid_of(positive), grid_of(account_ids), grid_of(merchant_ids),
        account_owner.reshape(1, blocks), merchant_owner.reshape(1, blocks), logit_scale, logit_bias,
    )


def solution(mesh):
    return jax.shard_map(
        functools.partial(per_device, mesh.shape["blk"]),
        mesh=mesh,
        in_specs=(
            P(("blk", "tab"), None),
            P(("blk", "tab"), None),
            P(),
            P(),
            P(("blk", "tab")),
            P(("blk", "tab")),
            P(("blk", "tab")),
            P(("blk", "tab"), None),
            P(("blk", "tab"), None),
        ),
        out_specs=(P(("blk", "tab"), None), P(("blk", "tab"), None)),
        check_vma=False,
    )
```
